32 devices in a mesh: pb: 4 (over y, core), ctx: 8 (over z, x).
Axes of the slice: x: 2, y: 2, z: 4, core: 2. Of those that a mesh axis runs over, the one named last changes fastest.
Arguments:
- queries: bfloat16 [32768, 1024], P(('pb', 'ctx')), may hold values from -64 to 64
- key_states: bfloat16 [32768, 128], P(('pb', 'ctx')), may hold values from -6 to 6
- value_states: bfloat16 [32768, 128], P(('pb', 'ctx')), may hold values from -6 to 6
- key_blocks: int32 [256, 8], replicated, may hold values from -1 to 255, as said below
Outputs:
- attended: bfloat16 [32768, 1024], P(('pb', 'ctx'))
The draws below stay inside these ranges and needn't reach their ends.
Inputs may be any that keep to these rules, and one draw needn't show every extreme that they name: `key_blocks`: row i lists first the blocks 0 to 1, then those of blocks i - 1, i, i + 1 that exist and are not among them, in increasing order, then 3 distinct blocks of other devices with the same pb index, none among those already listed and none next to the device's own 8 blocks; -1 fills the rest. Over the 8 rows of one device, at most 4 of the random entries name blocks of any one other device, and every device reaches that.
All inputs are finite; a program needn't handle non-finite values.
Results may differ from the reference program's by a relative error of at most 0.0047.
Values may be sent and summed in bfloat16 or wider, within the bound.
No kernel may reach another device: no remote copies, remote signals or barrier semaphores. Data moves between devices by JAX's collectives and lax.ppermute only.
A program may use at most 128 MiB of HBM per device.

```python
import jax
import jax.numpy as jnp
from jax import lax

HEAD_DIM = 128
HEADS = 8
BLOCK = 128
QBLOCKS = 8
GLOBAL = 2
RANDOM = 3
LIST = 8
NBLOCKS = 256
SEQ_LEN = 32768
N_CTX = 8


def base_keys(key):
    drawn_key = jax.random.fold_in(key, 7)
    drawn = jnp.clip(jax.random.normal(drawn_key, (SEQ_LEN, HEAD_DIM), jnp.float32), -6.0, 6.0)
    return drawn


def draw_key_states(key, part):
    drawn = base_keys(key)
    return drawn.astype(jnp.bfloat16)


def draw_queries(key, part):
    drawn_key = jax.random.fold_in(key, 13)
    drawn = jnp.clip(jax.random.normal(drawn_key, (SEQ_LEN, HEADS, HEAD_DIM), jnp.float32), -6.0, 6.0)
    return drawn.reshape(SEQ_LEN, HEADS * HEAD_DIM).astype(jnp.bfloat16)


def draw_key_blocks(key, part):
    devices_all = NBLOCKS // QBLOCKS
    others = N_CTX - 1
    rows_all = jnp.arange(NBLOCKS, dtype=jnp.int32)
    device_of = rows_all // QBLOCKS
    within_dev = rows_all % QBLOCKS
    column = device_of % N_CTX
    first_block = device_of * QBLOCKS
    owner_score = jax.random.randint(jax.random.fold_in(key, 3), (devices_all, others), 0, 65536) * others + jnp.arange(others, dtype=jnp.int32)[None, :]
    owner_perm = jnp.argsort(owner_score, axis=1).astype(jnp.int32)
    entry_number = within_dev[:, None] * RANDOM + jnp.arange(RANDOM, dtype=jnp.int32)[None, :]
    picked = jnp.take_along_axis(owner_perm[device_of], entry_number % others, axis=1)
    holder = (column[:, None] + 1 + picked) % N_CTX
    holder_dev = (device_of // N_CTX * N_CTX)[:, None] + holder
    candidates = holder_dev[:, :, None] * QBLOCKS + jnp.arange(QBLOCKS, dtype=jnp.int32)[None, None, :]
    lower = (first_block - 1)[:, None, None]
    upper = (first_block + QBLOCKS)[:, None, None]
    forbidden = ((candidates < GLOBAL) | (candidates >= lower) & (candidates <= upper)).astype(jnp.int32)
    pick_score = jax.random.randint(jax.random.fold_in(key, 5), (NBLOCKS, RANDOM, QBLOCKS), 0, 65536) * QBLOCKS
    pick_score = pick_score + jnp.arange(QBLOCKS, dtype=jnp.int32)[None, None, :] + forbidden * (1 << 26)
    chosen = jnp.argmin(pick_score, axis=2).astype(jnp.int32)
    random_blocks = holder_dev * QBLOCKS + chosen
    window_blocks = rows_all[:, None] + jnp.arange(-1, 2, dtype=jnp.int32)[None, :]
    window_ok = (window_blocks >= GLOBAL) & (window_blocks < NBLOCKS)
    window_pos = jnp.where(window_ok, GLOBAL + jnp.cumsum(window_ok.astype(jnp.int32), axis=1) - 1, -5)
    window_count = jnp.sum(window_ok.astype(jnp.int32), axis=1)
    random_pos = GLOBAL + window_count[:, None] + jnp.arange(RANDOM, dtype=jnp.int32)[None, :]
    global_pos = jnp.broadcast_to(jnp.arange(GLOBAL, dtype=jnp.int32)[None, :], (NBLOCKS, GLOBAL))
    global_blocks = global_pos
    positions = jnp.concatenate([global_pos, window_pos, random_pos], axis=1)
    entries = jnp.concatenate([global_blocks, window_blocks, random_blocks], axis=1)
    slots = jnp.arange(LIST, dtype=jnp.int32)
    placed = (positions[:, :, None] == slots[None, None, :]).astype(jnp.int32)
    listed = jnp.sum(placed * (entries[:, :, None] + 1), axis=1) - 1
    return listed.astype(jnp.int32)


def steps_of(rng, shape, split, low, high):
    gain, own = 1.0, jax.random.fold_in(rng, 6)
    for dim, blocks in split:
        heights = jnp.exp(jax.random.uniform(jax.random.fold_in(own, dim), (blocks,), jnp.float32, low / len(split), high / len(split)))
        gain = gain * jnp.repeat(heights, shape[dim] // blocks).reshape([-1 if axis == dim else 1 for axis in range(len(shape))])
    return gain


def bell_draw(stream_key, shape, deviation, most, pieces=(), held_as=jnp.bfloat16):
    factor_of = steps_of(stream_key, shape, pieces, -0.22, 0.18) if pieces else 1.0
    array = jax.random.normal(stream_key, shape, jnp.float32) * deviation * factor_of
    return jnp.minimum(jnp.maximum(array, -most), most).astype(held_as)


def setup_inputs(seed: int = 0) -> dict:
    key_list = jax.random.split(jax.random.key(seed), 5)
    return {
        "queries": draw_queries(jax.random.fold_in(key_list[4], 71), 0),
        "key_states": draw_key_states(jax.random.fold_in(key_list[4], 71), 0),
        "value_states": bell_draw(key_list[2], (SEQ_LEN, HEAD_DIM), 1.0, 6.0, ((0, 32),)),
        "key_blocks": draw_key_blocks(jax.random.fold_in(key_list[4], 71), 0),
    }


def attend(query_block, key_rows, value_rows, key_mask):
    scores = jnp.einsum("thd,ud->thu", query_block.astype(jnp.float32), key_rows.astype(jnp.float32)) * (HEAD_DIM ** -0.5)
    scores = jnp.where(key_mask[None, None, :], scores, -1e30)
    row_max = jnp.max(scores, axis=-1, keepdims=True)
    weights = jnp.exp(scores - row_max)
    normalizer = jnp.sum(weights, axis=-1, keepdims=True)
    rounded = weights.astype(jnp.bfloat16)
    result = jnp.einsum("thu,ud->thd", rounded.astype(jnp.float32), value_rows.astype(jnp.float32)) / normalizer
    return result.astype(jnp.bfloat16)


def reference(queries, key_states, value_states, key_blocks):
    key_cube = key_states.reshape(NBLOCKS, BLOCK, HEAD_DIM)
    value_cube = value_states.reshape(NBLOCKS, BLOCK, HEAD_DIM)
    query_cube = queries.reshape(NBLOCKS, BLOCK, HEADS, HEAD_DIM)

    def per_block(inputs):
        query_block, listed = inputs
        usable = listed >= 0
        safe_list = jnp.where(usable, listed, 0).astype(jnp.int32)
        key_rows = key_cube[safe_list].reshape(LIST * BLOCK, HEAD_DIM)
        value_rows = value_cube[safe_list].reshape(LIST * BLOCK, HEAD_DIM)
        key_mask = jnp.repeat(usable, BLOCK)
        return attend(query_block, key_rows, value_rows, key_mask)

    result = lax.map(per_block, (query_cube, key_blocks))
    return result.reshape(SEQ_LEN, HEADS * HEAD_DIM)
```

```python
import jax
import jax.numpy as jnp
from jax import lax
from jax.experimental import pallas as pl
from jax.experimental.pallas import tpu as pltpu
from jax.sharding import PartitionSpec as P

HEAD_DIM = 128
HEADS = 8
BLOCK = 128
GLOBAL = 2
RANDOM = 3
LIST = 8
COST = 1 << 30
CHUNK = 4
TO_LOG2 = HEAD_DIM**-0.5 * 1.4426950408889634

VMEM = pl.BlockSpec(memory_space=pltpu.VMEM)
SMEM = pl.BlockSpec(memory_space=pltpu.SMEM)


def random_start(row, n_blocks):
    low = jnp.maximum(row - 1, GLOBAL)
    high = jnp.minimum(row + 1, n_blocks - 1)
    return GLOBAL + high - low + 1


def group_rows(key_blocks):
    n_rows = key_blocks.shape[0] // lax.axis_size("pb")
    return lax.dynamic_slice_in_dim(
        key_blocks, lax.axis_index("pb") * n_rows, n_rows, 0
    ).reshape(-1)


def ring_of(n_ctx):
    return list(range(0, n_ctx, 2)) + list(range(n_ctx - 1, 0, -2))


def place_of(index, n_ctx):
    return jnp.where(index % 2 == 0, index // 2, n_ctx - 1 - index // 2)


def device_at(place, n_ctx):
    place = lax.rem(place + n_ctx, n_ctx)
    return jnp.where(place < n_ctx // 2, 2 * place, 2 * (n_ctx - 1 - place) + 1)


def plan_kernel(sizes, list_ref, plan_ref, counts):
    n_pb, n_ctx, n_dev, slots = sizes
    n_blocks = n_pb * n_ctx * n_dev
    me = lax.axis_index("ctx")
    group = lax.axis_index("pb") * (n_ctx * n_dev)
    place = place_of(me, n_ctx)
    half = slots // 2
    spare = 2 * (slots + half) + n_dev * RANDOM

    def entry(device, r, j):
        row = device * n_dev + r
        return list_ref[row * LIST + random_start(group + row, n_blocks) + j]

    for side, sign in enumerate((1, -1)):
        base = side * (slots + half)
        source = device_at(place - 2 * sign, n_ctx)
        first = group + source * n_dev
        for i in range(slots + half):
            plan_ref[base + i] = 0
        for steps, low, high, at in ((2, side * half, (side + 1) * half, 0), (1, 0, slots, half)):
            target = device_at(place + steps * sign, n_ctx)
            count = jnp.int32(0)
            for r in range(n_dev):
                for j in range(RANDOM):
                    local = entry(target, r, j) - first
                    hit = jnp.logical_and(local >= 0, local < n_dev)
                    use = jnp.logical_and(hit, jnp.logical_and(count >= low, count < high))
                    plan_ref[jnp.where(use, base + at + count - low, spare)] = local
                    count = count + hit.astype(jnp.int32)
    for h in range(n_ctx):
        counts[h] = 0
    for r in range(n_dev):
        for j in range(RANDOM):
            block = entry(me, r, j) - group
            holder = block // n_dev
            local = block - holder * n_dev
            rank = counts[holder]
            counts[holder] = rank + 1
            away = lax.rem(place - place_of(holder, n_ctx) + n_ctx, n_ctx)
            whole = jnp.where(away <= 2, away - 1, n_ctx + 1 - away) * n_dev + local
            few = jnp.where(away == 4, 0, jnp.where(away == 3, slots, 2 * slots)) + rank
            is_few = jnp.logical_and(away >= 3, away <= 5)
            plan_ref[2 * (slots + half) + r * RANDOM + j] = jnp.where(is_few, 4 * n_dev + few, whole)


def make_plan(sizes, lists):
    n_pb, n_ctx, n_dev, slots = sizes
    length = 2 * (slots + slots // 2) + n_dev * RANDOM + 1
    return pl.pallas_call(
        lambda *refs: plan_kernel(sizes, *refs),
        out_shape=jax.ShapeDtypeStruct((length,), jnp.int32),
        in_specs=[SMEM],
        out_specs=SMEM,
        scratch_shapes=[pltpu.SMEM((n_ctx,), jnp.int32)],
        name="plan",
    )(lists)


def pick_kernel(base, half, slots, plan_ref, k_ref, v_ref, far_ref, out_ref):
    for ref, at, n in ((far_ref, base, half), (out_ref, base + half, slots)):
        for s in range(n):
            ref[s, 0] = k_ref[plan_ref[at + s]]
            ref[s, 1] = v_ref[plan_ref[at + s]]


def pick(sizes, side, plan, keys, values):
    slots = sizes[3]
    half = slots // 2
    return pl.pallas_call(
        lambda *refs: pick_kernel(side * (slots + half), half, slots, *refs),
        out_shape=[
            jax.ShapeDtypeStruct((n, 2, BLOCK, HEAD_DIM), jnp.bfloat16) for n in (half, slots)
        ],
        in_specs=[SMEM, VMEM, VMEM],
        out_specs=[VMEM, VMEM],
        name="pick",
    )(plan, keys, values)


def pass_round(sizes, plan, keys, values):
    n_ctx, n_dev, slots = sizes[1:]
    half = slots // 2
    ring = ring_of(n_ctx)
    parts = []
    for side in range(2):
        step = 1 if side == 0 else -1
        pairs = [(ring[i], ring[(i + step) % n_ctx]) for i in range(n_ctx)]
        k, v = keys, values
        for hop in range(2):
            k, v = lax.ppermute(k, "ctx", pairs), lax.ppermute(v, "ctx", pairs)
            at = (2 * side + hop) * n_dev
            parts += [(k, at, 0), (v, at, 1)]
        onward, near = pick(sizes, side, plan, k, v)
        onward = lax.ppermute(onward, "ctx", pairs)
        near = lax.ppermute(near, "ctx", pairs)
        opposite = lax.ppermute(onward, "ctx", pairs)
        parts += [(opposite, 4 * n_dev + side * half, None), (near, 4 * n_dev + (1 + side) * slots, None)]
    return parts


def gather_kernel(sizes, list_ref, k_ref, v_ref, *rest):
    n_pb, n_ctx, n_dev, slots = sizes
    outs, table = rest[:-1], rest[-1]
    n_blocks = n_pb * n_ctx * n_dev
    me = lax.axis_index("ctx")
    group = lax.axis_index("pb") * (n_ctx * n_dev)
    own = group + me * n_dev
    for i in range((n_ctx - 1) * slots + 1):
        table[i] = 0
    for shift in range(1, n_ctx):
        first = lax.rem(me + shift, n_ctx) * n_dev
        count = jnp.int32(0)
        for r in range(n_dev):
            row = first + r
            start = row * LIST + random_start(group + row, n_blocks)
            for j in range(RANDOM):
                local = list_ref[start + j] - own
                hit = jnp.logical_and(local >= 0, local < n_dev)
                place = jnp.where(hit, (shift - 1) * slots + count, (n_ctx - 1) * slots)
                table[place] = local
                count = count + hit.astype(jnp.int32)
    for shift in range(1, n_ctx):
        for s in range(slots):
            local = table[(shift - 1) * slots + s]
            outs[shift - 1][s, 0] = k_ref[local]
            outs[shift - 1][s, 1] = v_ref[local]


def gather(sizes, lists, key_states, value_states):
    n_pb, n_ctx, n_dev, slots = sizes
    return pl.pallas_call(
        lambda *refs: gather_kernel(sizes, *refs),
        out_shape=[jax.ShapeDtypeStruct((slots, 2, BLOCK, HEAD_DIM), jnp.bfloat16)] * (n_ctx - 1),
        in_specs=[SMEM, VMEM, VMEM],
        out_specs=[VMEM] * (n_ctx - 1),
        scratch_shapes=[pltpu.SMEM(((n_ctx - 1) * slots + 1,), jnp.int32)],
        name="gather",
    )(lists, key_states, value_states)


def softmax_part(q_ref, heads, keys, values):
    q = jnp.concatenate([q_ref[:, h * HEAD_DIM : (h + 1) * HEAD_DIM] for h in heads], axis=0)
    scores = lax.dot_general(
        q, keys[...], (((1,), (1,)), ((), ())), preferred_element_type=jnp.float32
    )
    top = jnp.max(scores, axis=1, keepdims=True)
    weights = jnp.exp2((scores - top) * TO_LOG2).astype(jnp.bfloat16)
    total = jnp.dot(weights, values[...], preferred_element_type=jnp.float32)
    return top * TO_LOG2, total[:, :HEAD_DIM], total[:, HEAD_DIM:]


def attend(q_ref, keys, values, before, out_ref, lse_ref):
    lane = lax.broadcasted_iota(jnp.int32, (BLOCK, HEAD_DIM), 1)
    earlier = None if before is None else before[1][...]
    packed = jnp.zeros((BLOCK, HEAD_DIM), jnp.float32)
    for c in range(0, HEADS, CHUNK):
        heads = range(c, c + CHUNK)
        tops, totals, norms = softmax_part(q_ref, heads, keys, values)
        for n, h in enumerate(heads):
            rows = slice(n * BLOCK, (n + 1) * BLOCK)
            lanes = slice(h * HEAD_DIM, (h + 1) * HEAD_DIM)
            top, total, norm = tops[rows], totals[rows], norms[rows]
            if before is not None:
                lse = jnp.max(jnp.where(lane == h, earlier, -jnp.inf), axis=1, keepdims=True)
                highest = jnp.maximum(lse, top)
                a, b = jnp.exp2(lse - highest), jnp.exp2(top - highest)
                total, norm, top = before[0][:, lanes] * a + total * b, a + norm * b, highest
            out_ref[:, lanes] = (total / norm).astype(out_ref.dtype)
            if lse_ref is not None:
                packed = jnp.where(lane == h, top + jnp.log2(norm), packed)
    if lse_ref is not None:
        lse_ref[...] = packed


def put(keys, values, slot, block, counts=None):
    rows = slice(slot * BLOCK, (slot + 1) * BLOCK)
    keys[rows, :] = block[0]
    value, one = block[1], jnp.ones((BLOCK, HEAD_DIM), jnp.bfloat16)
    if counts is not None:
        value = jnp.where(counts, value, jnp.zeros_like(value))
        one = jnp.where(counts, one, jnp.zeros_like(one))
    values[rows, :HEAD_DIM] = value
    values[rows, HEAD_DIM:] = one


def near_kernel(sizes, q_ref, k_ref, v_ref, before_ref, after_ref, global_ref, out_ref, lse_ref, keys, values):
    n_pb, n_ctx, n_dev, slots = sizes
    n_blocks = n_pb * n_ctx * n_dev
    i = pl.program_id(0)
    row = (lax.axis_index("pb") * n_ctx + lax.axis_index("ctx")) * n_dev + i
    for g in range(GLOBAL):
        put(keys, values, g, (global_ref[g, 0], global_ref[g, 1]))
    for slot, step in enumerate((-1, 0, 1), GLOBAL):
        counts = jnp.logical_and(row + step >= GLOBAL, row + step < n_blocks)
        inside = jnp.logical_and(i + step >= 0, i + step < n_dev)
        here = jnp.logical_and(counts, inside)

        @pl.when(here)
        def _():
            put(keys, values, slot, (k_ref[i + step], v_ref[i + step]))

        @pl.when(jnp.logical_not(counts))
        def _():
            put(keys, values, slot, (global_ref[0, 0], global_ref[0, 1]), False)

        if step != 0:
            other = before_ref if step < 0 else after_ref

            @pl.when(jnp.logical_and(counts, jnp.logical_not(inside)))
            def _():
                put(keys, values, slot, other[0])

    attend(q_ref, keys, values, None, out_ref, lse_ref)


def random_kernel(places, table_at, plan_ref, q_ref, o_ref, l_ref, *rest):
    parts, (out_ref, keys, values, pool, sems) = rest[: len(places)], rest[len(places) :]
    i = pl.program_id(0)

    @pl.when(i == 0)
    def _():
        copies = []
        for n, (part, (at, which)) in enumerate(zip(parts, places)):
            rows = pl.ds(at, part.shape[0])
            target = pool.at[rows] if which is None else pool.at[rows, which]
            copies.append(pltpu.make_async_copy(part, target, sems.at[n]))
        for copy in copies:
            copy.start()
        values[:, HEAD_DIM:] = jnp.ones((RANDOM * BLOCK, HEAD_DIM), jnp.bfloat16)
        for copy in copies:
            copy.wait()

    for j in range(RANDOM):
        block = plan_ref[table_at + i * RANDOM + j]
        rows = slice(j * BLOCK, (j + 1) * BLOCK)
        keys[rows, :] = pool[block, 0]
        values[rows, :HEAD_DIM] = pool[block, 1]
    attend(q_ref, keys, values, (o_ref, l_ref), out_ref, None)


def shift_plan_kernel(sizes, list_ref, plan_ref, counts):
    n_pb, n_ctx, n_dev, slots = sizes
    n_blocks = n_pb * n_ctx * n_dev
    me = lax.axis_index("ctx")
    group = lax.axis_index("pb") * (n_ctx * n_dev)
    for h in range(n_ctx):
        counts[h] = 0
    for r in range(n_dev):
        row = me * n_dev + r
        start = row * LIST + random_start(group + row, n_blocks)
        for j in range(RANDOM):
            holder = (list_ref[start + j] - group) // n_dev
            rank = counts[holder]
            counts[holder] = rank + 1
            shift = lax.rem(me - holder + n_ctx, n_ctx)
            plan_ref[r * RANDOM + j] = (shift - 1) * slots + rank


def shift_round(sizes, lists, keys, values):
    n_pb, n_ctx, n_dev, slots = sizes
    plan = pl.pallas_call(
        lambda *refs: shift_plan_kernel(sizes, *refs),
        out_shape=jax.ShapeDtypeStruct((n_dev * RANDOM,), jnp.int32),
        in_specs=[SMEM],
        out_specs=SMEM,
        scratch_shapes=[pltpu.SMEM((n_ctx,), jnp.int32)],
        name="plan",
    )(lists)
    parts = []
    for shift, part in enumerate(gather(sizes, lists, keys, values), 1):
        got = lax.ppermute(part, "ctx", [(i, (i + shift) % n_ctx) for i in range(n_ctx)])
        parts.append((got, (shift - 1) * slots, None))
    return plan, parts


def call(kernel, name, n_dev, scalars, tiled, whole, parts, n_blocks, last, cost, scratch=()):
    width = HEADS * HEAD_DIM

    def tile(n):
        return pl.BlockSpec((BLOCK, n), lambda i: (i, 0))

    out_shape = [jax.ShapeDtypeStruct((n_dev * BLOCK, width), jnp.bfloat16 if last else jnp.float32)]
    if not last:
        out_shape.append(jax.ShapeDtypeStruct((n_dev * BLOCK, HEAD_DIM), jnp.float32))
    return pl.pallas_call(
        kernel,
        grid=(n_dev,),
        out_shape=out_shape,
        in_specs=[SMEM] * len(scalars)
        + [tile(a.shape[1]) for a in tiled]
        + [VMEM] * len(whole)
        + [pl.BlockSpec(memory_space=pl.ANY)] * len(parts),
        out_specs=[tile(a.shape[1]) for a in out_shape],
        scratch_shapes=[
            pltpu.VMEM((n_blocks * BLOCK, HEAD_DIM), jnp.bfloat16),
            pltpu.VMEM((n_blocks * BLOCK, 2 * HEAD_DIM), jnp.bfloat16),
            *scratch,
        ],
        cost_estimate=pl.CostEstimate(flops=cost, transcendentals=0, bytes_accessed=0),
        name=name,
    )(*scalars, *tiled, *whole, *parts)


def neighbours(first, last):
    axes = ("pb", "ctx")
    n = lax.axis_size(axes)
    up = [(i, i + 1) for i in range(n - 1)]
    down = [(i + 1, i) for i in range(n - 1)]
    return lax.ppermute(last, axes, up), lax.ppermute(first, axes, down)


def spread(shared):
    n_ctx, n_pb = lax.axis_size("ctx"), lax.axis_size("pb")
    column, group = lax.axis_index("ctx"), lax.axis_index("pb")
    axes = ("pb", "ctx")
    received = [lax.ppermute(shared, axes, [(0, far)]) for far in range(2, n_ctx, 2)]
    for far, got in zip(range(2, n_ctx, 2), received):
        shared = jnp.where(column == far, got, shared)
    got = lax.ppermute(shared, axes, [(c, c + 1) for c in range(0, n_ctx, 2)])
    shared = jnp.where(column % 2 == 1, got, shared)
    have = 1
    while have < n_pb:
        pairs = [(i, i + have) for i in range(min(have, n_pb - have))]
        got = lax.ppermute(shared, "pb", pairs)
        shared = jnp.where(jnp.logical_and(group >= have, group < 2 * have), got, shared)
        have *= 2
    return shared


def per_device(queries, key_states, value_states, key_blocks):
    n_pb, n_ctx = lax.axis_size("pb"), lax.axis_size("ctx")
    n_dev = queries.shape[0] // BLOCK
    slots = (RANDOM * n_dev + n_ctx - 2) // (n_ctx - 1)
    sizes = (n_pb, n_ctx, n_dev, slots)
    keys = key_states.reshape(n_dev, BLOCK, HEAD_DIM)
    values = value_states.reshape(n_dev, BLOCK, HEAD_DIM)
    lists = group_rows(key_blocks)
    if n_ctx == 8:
        plan = make_plan(sizes, lists)
        table_at = 2 * (slots + slots // 2)
        parts = pass_round(sizes, plan, keys, values)
    else:
        table_at = 0
        plan, parts = shift_round(sizes, lists, keys, values)
    first = jnp.stack([keys[:GLOBAL], values[:GLOBAL]], axis=1)
    last = jnp.stack([keys[-1:], values[-1:]], axis=1)
    before, after = neighbours(first[:1], last)
    shared = spread(first)
    out, lse = call(
        lambda *refs: near_kernel(sizes, *refs), "near", n_dev, [], [queries],
        [keys, values, before, after, shared], [], GLOBAL + 3, False, COST,
    )
    places = [part[1:] for part in parts]
    n_pool = max(at + part.shape[0] for part, at, _ in parts)
    (out,) = call(
        lambda *refs: random_kernel(places, table_at, *refs), "random", n_dev, [plan], [queries, out, lse], [],
        [part[0] for part in parts], RANDOM, True, COST,
        scratch=[
            pltpu.VMEM((n_pool, 2, BLOCK, HEAD_DIM), jnp.bfloat16),
            pltpu.SemaphoreType.DMA((len(parts),)),
        ],
    )
    return out


def solution(mesh):
    in_specs = (P(("pb", "ctx"), None), P(("pb", "ctx"), None), P(("pb", "ctx"), None), P())
    out_specs = P(("pb", "ctx"), None)
    return jax.shard_map(
        per_device, mesh=mesh, in_specs=in_specs, out_specs=out_specs, check_vma=False
    )
```

```python
import jax
import jax.numpy as jnp
from jax import lax
from jax.experimental import pallas as pl
from jax.experimental.pallas import tpu as pltpu
from jax.sharding import PartitionSpec as P

HEAD_DIM = 128
HEADS = 8
BLOCK = 128
GLOBAL = 2
RANDOM = 3
LIST = 8
COST = (1 << 30, 1 << 30)
TO_LOG2 = HEAD_DIM**-0.5 * 1.4426950408889634

VMEM = pl.BlockSpec(memory_space=pltpu.VMEM)
SMEM = pl.BlockSpec(memory_space=pltpu.SMEM)


def random_start(row, n_blocks):
    low = jnp.maximum(row - 1, GLOBAL)
    high = jnp.minimum(row + 1, n_blocks - 1)
    return GLOBAL + high - low + 1


def group_rows(key_blocks):
    n_rows = key_blocks.shape[0] // lax.axis_size("pb")
    return lax.dynamic_slice_in_dim(
        key_blocks, lax.axis_index("pb") * n_rows, n_rows, 0
    ).reshape(-1)


def ring_of(n_ctx):
    return list(range(0, n_ctx, 2)) + list(range(n_ctx - 1, 0, -2))


def place_of(index, n_ctx):
    return jnp.where(index % 2 == 0, index // 2, n_ctx - 1 - index // 2)


def edges(keys, values):
    n_dev = keys.shape[0]

    def kernel(k_first, v_first, k_last, v_last, shared_ref, first_ref, last_ref):
        for which, (first, last) in enumerate(((k_first, k_last), (v_first, v_last))):
            for g in range(GLOBAL):
                shared_ref[g, which] = first[g]
            first_ref[0, which] = first[0]
            last_ref[0, which] = last[0]

    head = pl.BlockSpec((GLOBAL, BLOCK, HEAD_DIM), lambda i: (0, 0, 0))
    tail = pl.BlockSpec((1, BLOCK, HEAD_DIM), lambda i: (n_dev - 1, 0, 0))
    return pl.pallas_call(
        kernel,
        grid=(1,),
        out_shape=[
            jax.ShapeDtypeStruct((n, 2, BLOCK, HEAD_DIM), jnp.bfloat16) for n in (GLOBAL, 1, 1)
        ],
        in_specs=[head, head, tail, tail],
        out_specs=[pl.BlockSpec((n, 2, BLOCK, HEAD_DIM), lambda i: (0, 0, 0, 0)) for n in (GLOBAL, 1, 1)],
        compiler_params=pltpu.CompilerParams(vmem_limit_bytes=2 << 20),
        name="edges",
    )(keys, values, keys, values)


def pass_round(keys, values):
    n_ctx = lax.axis_size("ctx")
    ring = ring_of(n_ctx)
    ahead = [(ring[i], ring[(i + 1) % n_ctx]) for i in range(n_ctx)]
    back = [(b, a) for a, b in ahead]
    parts = {}
    k = [keys, keys]
    v = [values, values]
    for hop in range(1, n_ctx // 2):
        for side, pairs in enumerate((ahead, back)):
            k[side] = lax.ppermute(k[side], "ctx", pairs)
        for side, pairs in enumerate((ahead, back)):
            v[side] = lax.ppermute(v[side], "ctx", pairs)
        parts[hop], parts[n_ctx - hop] = (k[0], v[0]), (k[1], v[1])
    parts[n_ctx // 2] = (lax.ppermute(k[0], "ctx", ahead), lax.ppermute(v[1], "ctx", back))
    return [parts[away] for away in range(1, n_ctx)]


def gather_kernel(sizes, list_ref, k_ref, v_ref, *rest):
    n_pb, n_ctx, n_dev, slots = sizes
    outs, table = rest[:-1], rest[-1]
    n_blocks = n_pb * n_ctx * n_dev
    me = lax.axis_index("ctx")
    group = lax.axis_index("pb") * (n_ctx * n_dev)
    own = group + me * n_dev
    for i in range((n_ctx - 1) * slots + 1):
        table[i] = 0
    for shift in range(1, n_ctx):
        first = lax.rem(me + shift, n_ctx) * n_dev
        count = jnp.int32(0)
        for r in range(n_dev):
            row = first + r
            start = row * LIST + random_start(group + row, n_blocks)
            for j in range(RANDOM):
                local = list_ref[start + j] - own
                hit = jnp.logical_and(local >= 0, local < n_dev)
                place = jnp.where(hit, (shift - 1) * slots + count, (n_ctx - 1) * slots)
                table[place] = local
                count = count + hit.astype(jnp.int32)
    for shift in range(1, n_ctx):
        for s in range(slots):
            local = table[(shift - 1) * slots + s]
            outs[shift - 1][s, 0] = k_ref[local]
            outs[shift - 1][s, 1] = v_ref[local]


def gather(sizes, lists, key_states, value_states):
    n_pb, n_ctx, n_dev, slots = sizes
    return pl.pallas_call(
        lambda *refs: gather_kernel(sizes, *refs),
        out_shape=[jax.ShapeDtypeStruct((slots, 2, BLOCK, HEAD_DIM), jnp.bfloat16)] * (n_ctx - 1),
        in_specs=[SMEM, VMEM, VMEM],
        out_specs=[VMEM] * (n_ctx - 1),
        scratch_shapes=[pltpu.SMEM(((n_ctx - 1) * slots + 1,), jnp.int32)],
        name="gather",
    )(lists, key_states, value_states)


def attend(n_dev, q_ref, before, out_ref, lse_ref, load_keys, load_values, buffers):
    scores, weights, scales = buffers[:2], buffers[2:4], buffers[4:6]
    half = HEADS // 2

    def lanes(h):
        return slice(h * HEAD_DIM, (h + 1) * HEAD_DIM)

    def rows_of(i):
        return pl.ds(pl.multiple_of(i * BLOCK, BLOCK), BLOCK)

    def form_scores(i, side):
        q = jnp.concatenate([q_ref[rows_of(i), lanes(side * half + n)] for n in range(half)], axis=0)
        scores[side][...] = lax.dot_general(
            q, load_keys(i), (((1,), (1,)), ((), ())), preferred_element_type=jnp.float32
        )

    def form_weights(i, side):
        for n in range(half):
            part = slice(n * BLOCK, (n + 1) * BLOCK)
            score = scores[side][part, :]
            top = jnp.max(score, axis=1, keepdims=True) * TO_LOG2
            if before is not None:
                lse = before[1][rows_of(i), lanes(side * half + n)]
                top = jnp.maximum(lse, top)
                scales[side][part, :] = jnp.exp2(lse - top)
                top = top[:, :1]
            else:
                scales[side][part, :] = jnp.broadcast_to(top, (BLOCK, HEAD_DIM))
            weights[side][part, :] = jnp.exp2(score * TO_LOG2 - top).astype(jnp.bfloat16)

    def sum_up(i, side):
        total = jnp.dot(weights[side][...], load_values(i), preferred_element_type=jnp.float32)
        for n in range(half):
            part = slice(n * BLOCK, (n + 1) * BLOCK)
            at = lanes(side * half + n)
            out, norm, scale = total[part, :HEAD_DIM], total[part, HEAD_DIM:], scales[side][part, :]
            if before is not None:
                out, norm = before[0][rows_of(i), at] * scale + out, scale + norm
            out_ref[rows_of(i), at] = (out / norm).astype(out_ref.dtype)
            if lse_ref is not None:
                lse_ref[rows_of(i), at] = scale + jnp.log2(norm)

    def step(u, _):
        now, last = jnp.minimum(u, n_dev - 1), jnp.maximum(u - 1, 0)
        form_scores(now, 0)
        form_weights(last, 1)
        sum_up(last, 0)
        form_scores(now, 1)
        form_weights(now, 0)
        sum_up(last, 1)
        return 0

    lax.fori_loop(0, n_dev + 1, step, 0)


def near_kernel(sizes, q_ref, k_ref, v_ref, before_ref, after_ref, global_ref, out_ref, lse_ref, pool, *buffers):
    n_pb, n_ctx, n_dev, slots = sizes
    n_blocks = n_pb * n_ctx * n_dev
    first = (lax.axis_index("pb") * n_ctx + lax.axis_index("ctx")) * n_dev
    shared = n_dev + 2
    pool[0] = before_ref[0]
    pool[1 : n_dev + 1, 0] = k_ref[...]
    pool[1 : n_dev + 1, 1] = v_ref[...]
    pool[n_dev + 1] = after_ref[0]
    pool[shared : shared + GLOBAL] = global_ref[...]

    def listed(i, step):
        block = first + i + step
        return jnp.logical_and(block >= GLOBAL, block < n_blocks)

    def load_keys(i):
        near = [pool[jnp.where(listed(i, step), i + 1 + step, shared), 0] for step in (-1, 0, 1)]
        return jnp.concatenate([pool[shared + g, 0] for g in range(GLOBAL)] + near, axis=0)

    def load_values(i):
        one = jnp.ones((BLOCK, HEAD_DIM), jnp.bfloat16)
        parts = [jnp.concatenate([pool[shared + g, 1], one], axis=1) for g in range(GLOBAL)]
        for step in (-1, 0, 1):
            part = jnp.concatenate([pool[i + 1 + step, 1], one], axis=1)
            parts.append(jnp.where(listed(i, step), part, jnp.zeros_like(part)))
        return jnp.concatenate(parts, axis=0)

    attend(n_dev, q_ref, None, out_ref, lse_ref, load_keys, load_values, buffers)


def random_kernel(sizes, where, list_ref, q_ref, o_ref, l_ref, *rest):
    n_pb, n_ctx, n_dev, slots = sizes
    parts, (out_ref, pool, table, counts, sems, *buffers) = rest[: len(where)], rest[len(where) :]
    copies = []
    for n, (part, (at, which)) in enumerate(zip(parts, where)):
        rows = pl.ds(at, part.shape[0])
        target = pool.at[rows] if which is None else pool.at[rows, which]
        copies.append(pltpu.make_async_copy(part, target, sems.at[n]))
    for copy in copies:
        copy.start()
    n_blocks = n_pb * n_ctx * n_dev
    me = lax.axis_index("ctx")
    group = lax.axis_index("pb") * (n_ctx * n_dev)
    whole = where[0][1] is not None
    for h in range(n_ctx):
        counts[h] = 0
    for r in range(n_dev):
        row = me * n_dev + r
        start = row * LIST + random_start(group + row, n_blocks)
        for j in range(RANDOM):
            block = list_ref[start + j] - group
            holder = block // n_dev
            if whole:
                away = lax.rem(place_of(me, n_ctx) - place_of(holder, n_ctx) + n_ctx, n_ctx)
                table[r * RANDOM + j] = (away - 1) * n_dev + block - holder * n_dev
            else:
                rank = counts[holder]
                counts[holder] = rank + 1
                table[r * RANDOM + j] = (lax.rem(me - holder + n_ctx, n_ctx) - 1) * slots + rank
    for copy in copies:
        copy.wait()

    def load_keys(i):
        return jnp.concatenate([pool[table[i * RANDOM + j], 0] for j in range(RANDOM)], axis=0)

    def load_values(i):
        values = jnp.concatenate([pool[table[i * RANDOM + j], 1] for j in range(RANDOM)], axis=0)
        return jnp.concatenate([values, jnp.ones_like(values)], axis=1)

    attend(n_dev, q_ref, (o_ref, l_ref), out_ref, None, load_keys, load_values, buffers)


def call(kernel, name, out_shape, scalars, whole, parts, n_keys, cost, scratch):
    rows = HEADS // 2 * BLOCK
    return pl.pallas_call(
        kernel,
        out_shape=out_shape,
        in_specs=[SMEM] * len(scalars)
        + [VMEM] * len(whole)
        + [pl.BlockSpec(memory_space=pl.ANY)] * len(parts),
        out_specs=[VMEM] * len(out_shape),
        scratch_shapes=[
            *scratch,
            *[pltpu.VMEM((rows, n_keys * BLOCK), jnp.float32)] * 2,
            *[pltpu.VMEM((rows, n_keys * BLOCK), jnp.bfloat16)] * 2,
            *[pltpu.VMEM((rows, HEAD_DIM), jnp.float32)] * 2,
        ],
        compiler_params=pltpu.CompilerParams(vmem_limit_bytes=20 << 20),
        cost_estimate=pl.CostEstimate(flops=cost, transcendentals=0, bytes_accessed=0),
        name=name,
    )(*scalars, *whole, *parts)


def shift_round(sizes, lists, keys, values):
    n_ctx = sizes[1]
    return [
        lax.ppermute(part, "ctx", [(i, (i + shift) % n_ctx) for i in range(n_ctx)])
        for shift, part in enumerate(gather(sizes, lists, keys, values), 1)
    ]


def neighbours(first, last):
    axes = ("pb", "ctx")
    n = lax.axis_size(axes)
    up = [(i, i + 1) for i in range(n - 1)]
    down = [(i + 1, i) for i in range(n - 1)]
    return lax.ppermute(last, axes, up), lax.ppermute(first, axes, down)


def spread(shared):
    n_ctx, n_pb = lax.axis_size("ctx"), lax.axis_size("pb")
    column, group = lax.axis_index("ctx"), lax.axis_index("pb")

    def fan(shared, axes, index, targets):
        received = [lax.ppermute(shared, axes, [(0, target)]) for target in targets]
        for target, got in zip(targets, received):
            shared = jnp.where(index == target, got, shared)
        return shared

    shared = fan(shared, ("pb", "ctx"), column, range(2, n_ctx, 2))
    got = lax.ppermute(shared, ("pb", "ctx"), [(c, c + 1) for c in range(0, n_ctx, 2)])
    shared = jnp.where(column % 2 == 1, got, shared)
    return fan(shared, "pb", group, range(1, n_pb))


def per_device(queries, key_states, value_states, key_blocks):
    n_pb, n_ctx = lax.axis_size("pb"), lax.axis_size("ctx")
    n_dev = queries.shape[0] // BLOCK
    slots = (RANDOM * n_dev + n_ctx - 2) // (n_ctx - 1)
    sizes = (n_pb, n_ctx, n_dev, slots)
    keys = key_states.reshape(n_dev, BLOCK, HEAD_DIM)
    values = value_states.reshape(n_dev, BLOCK, HEAD_DIM)
    lists = group_rows(key_blocks)
    if n_ctx == 8:
        parts, where = [], []
        for n, pair in enumerate(pass_round(keys, values)):
            parts += pair
            where += [(n * n_dev, 0), (n * n_dev, 1)]
    else:
        parts = shift_round(sizes, lists, keys, values)
        where = [(n * slots, None) for n in range(n_ctx - 1)]
    shared, first, last = edges(keys, values)
    before, after = neighbours(first, last)
    shared = spread(shared)
    return attention(sizes, queries, keys, values, before, after, shared, lists, where, parts)


def attention(sizes, queries, keys, values, before, after, shared, lists, where, parts):
    n_dev = sizes[2]
    partial = jax.ShapeDtypeStruct(queries.shape, jnp.float32)
    out, lse = call(
        lambda *refs: near_kernel(sizes, *refs), "near", [partial] * 2, [],
        [queries, keys, values, before, after, shared], [], GLOBAL + 3, COST[0],
        [pltpu.VMEM((n_dev + 2 + GLOBAL, 2, BLOCK, HEAD_DIM), jnp.bfloat16)],
    )
    n_pool = max(at + part.shape[0] for part, (at, _) in zip(parts, where))
    (out,) = call(
        lambda *refs: random_kernel(sizes, where, *refs), "random",
        [jax.ShapeDtypeStruct(queries.shape, jnp.bfloat16)], [lists], [queries, out, lse], parts, RANDOM, COST[1],
        [
            pltpu.VMEM((n_pool, 2, BLOCK, HEAD_DIM), jnp.bfloat16),
            pltpu.SMEM((n_dev * RANDOM,), jnp.int32),
            pltpu.SMEM((sizes[1],), jnp.int32),
            pltpu.SemaphoreType.DMA((len(parts),)),
        ],
    )
    return out


def solution(mesh):
    in_specs = (P(("pb", "ctx"), None), P(("pb", "ctx"), None), P(("pb", "ctx"), None), P())
    out_specs = P(("pb", "ctx"), None)
    return jax.shard_map(
        per_device, mesh=mesh, in_specs=in_specs, out_specs=out_specs, check_vma=False
    )
```

```python
import jax
import jax.numpy as jnp
from jax import lax
from jax.experimental import pallas as pl
from jax.experimental.pallas import tpu as pltpu
from jax.sharding import PartitionSpec as P

HEAD_DIM = 128
HEADS = 8
BLOCK = 128
GLOBAL = 2
RANDOM = 3
LIST = 8
TO_LOG2 = HEAD_DIM**-0.5 * 1.4426950408889634

VMEM = pl.BlockSpec(memory_space=pltpu.VMEM)
MEM = pl.BlockSpec(memory_space=pltpu.HBM)
SMEM = pl.BlockSpec(memory_space=pltpu.SMEM)


def random_start(row, n_blocks):
    low = jnp.maximum(row - 1, GLOBAL)
    high = jnp.minimum(row + 1, n_blocks - 1)
    return GLOBAL + high - low + 1


def group_rows(key_blocks):
    n_rows = key_blocks.shape[0] // lax.axis_size("pb")
    return lax.dynamic_slice_in_dim(
        key_blocks, lax.axis_index("pb") * n_rows, n_rows, 0
    ).reshape(-1)


def ring_of(n_ctx):
    return list(range(0, n_ctx, 2)) + list(range(n_ctx - 1, 0, -2))


def place_of(index, n_ctx):
    return jnp.where(index % 2 == 0, index // 2, n_ctx - 1 - index // 2)


def edges(keys, values):
    n_dev = keys.shape[0]

    def kernel(k_ref, v_ref, first_ref, edge_ref, sems):
        last = lax.axis_index("ctx") == lax.axis_size("ctx") - 1
        edge = pl.ds(jnp.where(last, n_dev - 1, 0), 1)
        copies = []
        for which, ref in enumerate((k_ref, v_ref)):
            copies += [
                pltpu.make_async_copy(ref.at[pl.ds(0, GLOBAL)], first_ref.at[:, which], sems.at[2 * which]),
                pltpu.make_async_copy(ref.at[edge], edge_ref.at[:, which], sems.at[2 * which + 1]),
            ]
        for copy in copies:
            copy.start()
        for copy in copies:
            copy.wait()

    return pl.pallas_call(
        kernel,
        out_shape=[jax.ShapeDtypeStruct((n, 2, BLOCK, HEAD_DIM), jnp.bfloat16) for n in (GLOBAL, 1)],
        in_specs=[MEM, MEM],
        out_specs=[VMEM, VMEM],
        scratch_shapes=[pltpu.SemaphoreType.DMA((4,))],
        compiler_params=pltpu.CompilerParams(vmem_limit_bytes=2 << 20),
        name="edges",
    )(keys, values)


def first_of_group(first, direct, pairs):
    def kernel(*refs):
        *parts, out_ref, sems = refs
        place = place_of(lax.axis_index("ctx"), lax.axis_size("ctx"))
        for at, n in enumerate((0, 4)):

            @pl.when(place == n)
            def _():
                copy = pltpu.make_async_copy(parts[at], out_ref, sems.at[0])
                copy.start()
                copy.wait()

        for n, away in enumerate(whole):

            @pl.when(place == away)
            def _():
                copies = [
                    pltpu.make_async_copy(
                        parts[2 + 2 * n + which].at[pl.ds(0, GLOBAL)], out_ref.at[:, which], sems.at[which]
                    )
                    for which in range(2)
                ]
                for copy in copies:
                    copy.start()
                for copy in copies:
                    copy.wait()

    whole = [away for away in range(1, 8) if away != 4]
    parts = [first, direct] + [part for away in whole for part in pairs[away - 1]]
    return pl.pallas_call(
        kernel,
        out_shape=jax.ShapeDtypeStruct(first.shape, jnp.bfloat16),
        in_specs=[MEM] * len(parts),
        out_specs=VMEM,
        scratch_shapes=[pltpu.SemaphoreType.DMA((2,))],
        compiler_params=pltpu.CompilerParams(vmem_limit_bytes=2 << 20),
        name="first",
    )(*parts)


def pass_round(keys, values, small):
    n_ctx = lax.axis_size("ctx")
    ring = ring_of(n_ctx)
    ahead = [(ring[i], ring[(i + 1) % n_ctx]) for i in range(n_ctx)]
    back = [(b, a) for a, b in ahead]
    parts = {}
    k = [keys, keys]
    v = [values, values]
    for hop in range(1, n_ctx // 2):
        if hop == n_ctx // 2 - 1:
            k[0], small = lax.optimization_barrier((k[0], small))
        for side, pairs in enumerate((ahead, back)):
            k[side] = lax.ppermute(k[side], "ctx", pairs)
        for side, pairs in enumerate((ahead, back)):
            v[side] = lax.ppermute(v[side], "ctx", pairs)
        parts[hop], parts[n_ctx - hop] = (k[0], v[0]), (k[1], v[1])
    parts[n_ctx // 2] = (lax.ppermute(k[0], "ctx", ahead), lax.ppermute(v[1], "ctx", back))
    return [parts[away] for away in range(1, n_ctx)], small


def gather_kernel(sizes, list_ref, k_ref, v_ref, *rest):
    n_pb, n_ctx, n_dev, slots = sizes
    outs, table = rest[:-1], rest[-1]
    n_blocks = n_pb * n_ctx * n_dev
    me = lax.axis_index("ctx")
    group = lax.axis_index("pb") * (n_ctx * n_dev)
    own = group + me * n_dev
    for i in range((n_ctx - 1) * slots + 1):
        table[i] = 0
    for shift in range(1, n_ctx):
        first = lax.rem(me + shift, n_ctx) * n_dev
        count = jnp.int32(0)
        for r in range(n_dev):
            row = first + r
            start = row * LIST + random_start(group + row, n_blocks)
            for j in range(RANDOM):
                local = list_ref[start + j] - own
                hit = jnp.logical_and(local >= 0, local < n_dev)
                place = jnp.where(hit, (shift - 1) * slots + count, (n_ctx - 1) * slots)
                table[place] = local
                count = count + hit.astype(jnp.int32)
    for shift in range(1, n_ctx):
        for s in range(slots):
            local = table[(shift - 1) * slots + s]
            outs[shift - 1][s, 0] = k_ref[local]
            outs[shift - 1][s, 1] = v_ref[local]


def gather(sizes, lists, key_states, value_states):
    n_pb, n_ctx, n_dev, slots = sizes
    return pl.pallas_call(
        lambda *refs: gather_kernel(sizes, *refs),
        out_shape=[jax.ShapeDtypeStruct((slots, 2, BLOCK, HEAD_DIM), jnp.bfloat16)] * (n_ctx - 1),
        in_specs=[SMEM, VMEM, VMEM],
        out_specs=[VMEM] * (n_ctx - 1),
        scratch_shapes=[pltpu.SMEM(((n_ctx - 1) * slots + 1,), jnp.int32)],
        name="gather",
    )(lists, key_states, value_states)


def attend(n_dev, q_ref, out_ref, load_keys, load_values, buffers):
    scores, weights = buffers[:2], buffers[2:4]
    half = HEADS // 2

    def lanes(h):
        return slice(h * HEAD_DIM, (h + 1) * HEAD_DIM)

    def rows_of(i):
        return pl.ds(pl.multiple_of(i * BLOCK, BLOCK), BLOCK)

    def form_scores(i, side):
        q = jnp.concatenate([q_ref[rows_of(i), lanes(side * half + n)] for n in range(half)], axis=0)
        scores[side][...] = lax.dot_general(
            q, load_keys(i), (((1,), (1,)), ((), ())), preferred_element_type=jnp.float32
        )

    def form_weights(i, side):
        for n in range(half):
            part = slice(n * BLOCK, (n + 1) * BLOCK)
            score = scores[side][part, :]
            top = jnp.max(score, axis=1, keepdims=True)
            weights[side][part, :] = jnp.exp2((score - top) * TO_LOG2).astype(jnp.bfloat16)

    def sum_up(i, side):
        total = jnp.dot(weights[side][...], load_values(i), preferred_element_type=jnp.float32)
        for n in range(half):
            part = slice(n * BLOCK, (n + 1) * BLOCK)
            out = total[part, :HEAD_DIM] / total[part, HEAD_DIM:]
            out_ref[rows_of(i), lanes(side * half + n)] = out.astype(out_ref.dtype)

    form_scores(0, 0)
    form_scores(0, 1)
    form_weights(0, 0)

    def step(u, _):
        form_scores(u, 0)
        form_weights(u - 1, 1)
        sum_up(u - 1, 0)
        form_scores(u, 1)
        form_weights(u, 0)
        sum_up(u - 1, 1)
        return 0

    lax.fori_loop(1, n_dev, step, 0)
    form_weights(n_dev - 1, 1)
    sum_up(n_dev - 1, 0)
    sum_up(n_dev - 1, 1)


def attention_kernel(sizes, where, n_shared, list_ref, q_ref, k_ref, v_ref, before_ref, after_ref, *rest):
    n_pb, n_ctx, n_dev, slots = sizes
    shared_refs, rest = rest[:n_shared], rest[n_shared:]
    parts, (out_ref, pool, table, counts, sems, *buffers) = rest[: len(where)], rest[len(where) :]
    shared = n_dev + 2
    random = shared + GLOBAL
    copies = []
    for n, (part, (at, which)) in enumerate(zip(parts, where)):
        rows = pl.ds(random + at, part.shape[0])
        target = pool.at[rows] if which is None else pool.at[rows, which]
        copies.append(pltpu.make_async_copy(part, target, sems.at[n]))
    for copy in copies:
        copy.start()
    pool[0] = before_ref[0]
    pool[1 : n_dev + 1, 0] = k_ref[...]
    pool[1 : n_dev + 1, 1] = v_ref[...]
    pool[n_dev + 1] = after_ref[0]
    if n_shared == 1:
        pool[shared:random] = shared_refs[0][...]
    else:
        for p in range(n_shared):

            @pl.when(lax.axis_index("pb") == p)
            def _():
                pool[shared:random] = shared_refs[p][...]

    n_blocks = n_pb * n_ctx * n_dev
    me = lax.axis_index("ctx")
    group = lax.axis_index("pb") * (n_ctx * n_dev)
    first = group + me * n_dev

    def brought(block):
        holder = block // n_dev
        away = lax.rem(place_of(me, n_ctx) - place_of(holder, n_ctx) + n_ctx, n_ctx)
        return random + (away - 1) * n_dev + block - holder * n_dev

    ends = (jnp.int32(0), jnp.int32(n_dev + 1))
    if n_ctx == 8:
        own = me * n_dev
        ends = (
            jnp.where(me == 0, 0, brought(jnp.maximum(own - 1, 0))),
            jnp.where(me == n_ctx - 1, n_dev + 1, brought(jnp.minimum(own + n_dev, n_ctx * n_dev - 1))),
        )
    for h in range(n_ctx):
        counts[h] = 0
    for r in range(n_dev):
        row = me * n_dev + r
        start = row * LIST + random_start(group + row, n_blocks)
        for j in range(RANDOM):
            block = list_ref[start + j] - group
            if n_ctx == 8:
                table[r * RANDOM + j] = brought(block)
            else:
                holder = block // n_dev
                rank = counts[holder]
                counts[holder] = rank + 1
                table[r * RANDOM + j] = random + (lax.rem(me - holder + n_ctx, n_ctx) - 1) * slots + rank
    for copy in copies:
        copy.wait()

    def near(i, step):
        block = first + i + step
        place = jnp.where(i + step < 0, ends[0], jnp.where(i + step >= n_dev, ends[1], i + 1 + step))
        return place, jnp.logical_and(block >= GLOBAL, block < n_blocks)

    def load_keys(i):
        places = [shared + g for g in range(GLOBAL)]
        for step in (-1, 0, 1):
            place, use = near(i, step)
            places.append(jnp.where(use, place, shared))
        places += [table[i * RANDOM + j] for j in range(RANDOM)]
        return jnp.concatenate([pool[place, 0] for place in places], axis=0)

    def load_values(i):
        one = jnp.ones((BLOCK, HEAD_DIM), jnp.bfloat16)
        parts = [jnp.concatenate([pool[shared + g, 1], one], axis=1) for g in range(GLOBAL)]
        for step in (-1, 0, 1):
            place, use = near(i, step)
            part = jnp.concatenate([pool[jnp.where(use, place, shared), 1], one], axis=1)
            parts.append(jnp.where(use, part, jnp.zeros_like(part)))
        for j in range(RANDOM):
            parts.append(jnp.concatenate([pool[table[i * RANDOM + j], 1], one], axis=1))
        return jnp.concatenate(parts, axis=0)

    attend(n_dev, q_ref, out_ref, load_keys, load_values, buffers)


def attention(sizes, queries, keys, values, before, after, shared, lists, where, parts):
    n_dev = sizes[2]
    rows, n_keys = HEADS // 2 * BLOCK, (GLOBAL + 3 + RANDOM) * BLOCK
    n_pool = n_dev + 2 + GLOBAL + max(at + part.shape[0] for part, (at, _) in zip(parts, where))
    return pl.pallas_call(
        lambda *refs: attention_kernel(sizes, where, len(shared), *refs),
        out_shape=jax.ShapeDtypeStruct(queries.shape, jnp.bfloat16),
        in_specs=[SMEM] + [VMEM] * (5 + len(shared)) + [MEM] * len(parts),
        out_specs=VMEM,
        scratch_shapes=[
            pltpu.VMEM((n_pool, 2, BLOCK, HEAD_DIM), jnp.bfloat16),
            pltpu.SMEM((n_dev * RANDOM,), jnp.int32),
            pltpu.SMEM((sizes[1],), jnp.int32),
            pltpu.SemaphoreType.DMA((len(parts),)),
            *[pltpu.VMEM((rows, n_keys), jnp.float32)] * 2,
            *[pltpu.VMEM((rows, n_keys), jnp.bfloat16)] * 2,
        ],
        compiler_params=pltpu.CompilerParams(vmem_limit_bytes=24 << 20),
        name="attention",
    )(lists, queries, keys, values, before, after, *shared, *parts)


def shift_round(sizes, lists, keys, values):
    n_ctx = sizes[1]
    return [
        lax.ppermute(part, "ctx", [(i, (i + shift) % n_ctx) for i in range(n_ctx)])
        for shift, part in enumerate(gather(sizes, lists, keys, values), 1)
    ]


def neighbours(first, last):
    axes = ("pb", "ctx")
    n = lax.axis_size(axes)
    up = [(i, i + 1) for i in range(n - 1)]
    down = [(i + 1, i) for i in range(n - 1)]
    return lax.ppermute(last, axes, up), lax.ppermute(first, axes, down)


def spread(shared):
    n_ctx, n_pb = lax.axis_size("ctx"), lax.axis_size("pb")
    column, group = lax.axis_index("ctx"), lax.axis_index("pb")

    def fan(shared, axes, index, targets):
        received = [lax.ppermute(shared, axes, [(0, target)]) for target in targets]
        for target, got in zip(targets, received):
            shared = jnp.where(index == target, got, shared)
        return shared

    shared = fan(shared, ("pb", "ctx"), column, range(2, n_ctx, 2))
    got = lax.ppermute(shared, ("pb", "ctx"), [(c, c + 1) for c in range(0, n_ctx, 2)])
    shared = jnp.where(column % 2 == 1, got, shared)
    return fan(shared, "pb", group, range(1, n_pb))


def per_device(queries, key_states, value_states, key_blocks):
    n_pb, n_ctx = lax.axis_size("pb"), lax.axis_size("ctx")
    n_dev = queries.shape[0] // BLOCK
    slots = (RANDOM * n_dev + n_ctx - 2) // (n_ctx - 1)
    sizes = (n_pb, n_ctx, n_dev, slots)
    keys = key_states.reshape(n_dev, BLOCK, HEAD_DIM)
    values = value_states.reshape(n_dev, BLOCK, HEAD_DIM)
    lists = group_rows(key_blocks)
    first, edge = edges(keys, values)
    if n_ctx == 8:
        last = n_ctx - 1
        direct = lax.ppermute(first, ("pb", "ctx"), [(0, last)])
        across = [(p * n_ctx + last, (p + 1) * n_ctx) for p in range(n_pb - 1)]
        beside = lax.ppermute(edge, ("pb", "ctx"), across + [(b, a) for a, b in across])
        pairs, (direct, lists) = pass_round(keys, values, (direct, lists))
        before = after = beside
        parts = [part for pair in pairs for part in pair]
        where = [(n * n_dev, which) for n in range(n_ctx - 1) for which in range(2)]
        mine = first_of_group(first, direct, pairs)
        shared = [mine] + [lax.ppermute(mine, "pb", [(0, p)]) for p in range(1, n_pb)]
    else:
        parts = shift_round(sizes, lists, keys, values)
        where = [(n * slots, None) for n in range(n_ctx - 1)]
        last = jnp.stack([keys[-1:], values[-1:]], axis=1)
        before, after = neighbours(first[:1], last)
        shared = [spread(first)]
    return attention(sizes, queries, keys, values, before, after, shared, lists, where, parts)


def solution(mesh):
    in_specs = (P(("pb", "ctx"), None), P(("pb", "ctx"), None), P(("pb", "ctx"), None), P())
    out_specs = P(("pb", "ctx"), None)
    return jax.shard_map(
        per_device, mesh=mesh, in_specs=in_specs, out_specs=out_specs, check_vma=False
    )
```

```python
import jax
import jax.numpy as jnp
from jax import lax
from jax.experimental import pallas as pl
from jax.experimental.pallas import tpu as pltpu
from jax.sharding import PartitionSpec as P

HEAD_DIM = 128
HEADS = 8
BLOCK = 128
GLOBAL = 2
RANDOM = 3
LIST = 8
PARTS = 4
TO_LOG2 = HEAD_DIM**-0.5 * 1.4426950408889634

VMEM = pl.BlockSpec(memory_space=pltpu.VMEM)
MEM = pl.BlockSpec(memory_space=pltpu.HBM)
SMEM = pl.BlockSpec(memory_space=pltpu.SMEM)


def random_start(row, n_blocks):
    low = jnp.maximum(row - 1, GLOBAL)
    high = jnp.minimum(row + 1, n_blocks - 1)
    return GLOBAL + high - low + 1


def group_rows(key_blocks):
    n_rows = key_blocks.shape[0] // lax.axis_size("pb")
    return lax.dynamic_slice_in_dim(
        key_blocks, lax.axis_index("pb") * n_rows, n_rows, 0
    ).reshape(-1)


def ring_of(n_ctx):
    return list(range(0, n_ctx, 2)) + list(range(n_ctx - 1, 0, -2))


def place_of(index, n_ctx):
    return jnp.where(index % 2 == 0, index // 2, n_ctx - 1 - index // 2)


def edges(keys, values):
    n_dev = keys.shape[0]

    def kernel(k_ref, v_ref, first_ref, edge_ref, sems):
        last = lax.axis_index("ctx") == lax.axis_size("ctx") - 1
        edge = pl.ds(jnp.where(last, n_dev - 1, 0), 1)
        copies = []
        for which, ref in enumerate((k_ref, v_ref)):
            copies += [
                pltpu.make_async_copy(ref.at[pl.ds(0, GLOBAL)], first_ref.at[:, which], sems.at[2 * which]),
                pltpu.make_async_copy(ref.at[edge], edge_ref.at[:, which], sems.at[2 * which + 1]),
            ]
        for copy in copies:
            copy.start()
        for copy in copies:
            copy.wait()

    return pl.pallas_call(
        kernel,
        out_shape=[jax.ShapeDtypeStruct((n, 2, BLOCK, HEAD_DIM), jnp.bfloat16) for n in (GLOBAL, 1)],
        in_specs=[MEM, MEM],
        out_specs=[VMEM, VMEM],
        scratch_shapes=[pltpu.SemaphoreType.DMA((4,))],
        compiler_params=pltpu.CompilerParams(vmem_limit_bytes=2 << 20),
        name="edges",
    )(keys, values)


def first_of_group(first, direct, pairs):
    def kernel(*refs):
        *parts, out_ref, sems = refs
        place = place_of(lax.axis_index("ctx"), lax.axis_size("ctx"))
        for at, n in enumerate((0, 4)):

            @pl.when(place == n)
            def _():
                copy = pltpu.make_async_copy(parts[at], out_ref, sems.at[0])
                copy.start()
                copy.wait()

        for n, away in enumerate(whole):

            @pl.when(place == away)
            def _():
                copies = [
                    pltpu.make_async_copy(
                        parts[2 + 2 * n + which].at[pl.ds(0, GLOBAL)], out_ref.at[:, which], sems.at[which]
                    )
                    for which in range(2)
                ]
                for copy in copies:
                    copy.start()
                for copy in copies:
                    copy.wait()

    whole = [away for away in range(1, 8) if away != 4]
    parts = [first, direct] + [part for away in whole for part in pairs[away - 1]]
    return pl.pallas_call(
        kernel,
        out_shape=jax.ShapeDtypeStruct(first.shape, jnp.bfloat16),
        in_specs=[MEM] * len(parts),
        out_specs=VMEM,
        scratch_shapes=[pltpu.SemaphoreType.DMA((2,))],
        compiler_params=pltpu.CompilerParams(vmem_limit_bytes=2 << 20),
        name="first",
    )(*parts)


def pass_round(keys, values, small):
    n_ctx = lax.axis_size("ctx")
    ring = ring_of(n_ctx)
    ahead = [(ring[i], ring[(i + 1) % n_ctx]) for i in range(n_ctx)]
    back = [(b, a) for a, b in ahead]
    parts = {}
    k = [keys, keys]
    v = [values, values]
    for hop in range(1, n_ctx // 2):
        if hop == n_ctx // 2 - 1:
            k[0], small = lax.optimization_barrier((k[0], small))
        for side, pairs in enumerate((ahead, back)):
            k[side] = lax.ppermute(k[side], "ctx", pairs)
        for side, pairs in enumerate((ahead, back)):
            v[side] = lax.ppermute(v[side], "ctx", pairs)
        parts[hop], parts[n_ctx - hop] = (k[0], v[0]), (k[1], v[1])
    parts[n_ctx // 2] = (lax.ppermute(k[0], "ctx", ahead), lax.ppermute(v[1], "ctx", back))
    return [parts[away] for away in range(1, n_ctx)], small


def gather_kernel(sizes, list_ref, k_ref, v_ref, *rest):
    n_pb, n_ctx, n_dev, slots = sizes
    outs, table = rest[:-1], rest[-1]
    n_blocks = n_pb * n_ctx * n_dev
    me = lax.axis_index("ctx")
    group = lax.axis_index("pb") * (n_ctx * n_dev)
    own = group + me * n_dev
    for i in range((n_ctx - 1) * slots + 1):
        table[i] = 0
    for shift in range(1, n_ctx):
        first = lax.rem(me + shift, n_ctx) * n_dev
        count = jnp.int32(0)
        for r in range(n_dev):
            row = first + r
            start = row * LIST + random_start(group + row, n_blocks)
            for j in range(RANDOM):
                local = list_ref[start + j] - own
                hit = jnp.logical_and(local >= 0, local < n_dev)
                place = jnp.where(hit, (shift - 1) * slots + count, (n_ctx - 1) * slots)
                table[place] = local
                count = count + hit.astype(jnp.int32)
    for shift in range(1, n_ctx):
        for s in range(slots):
            local = table[(shift - 1) * slots + s]
            outs[shift - 1][s, 0] = k_ref[local]
            outs[shift - 1][s, 1] = v_ref[local]


def gather(sizes, lists, key_states, value_states):
    n_pb, n_ctx, n_dev, slots = sizes
    return pl.pallas_call(
        lambda *refs: gather_kernel(sizes, *refs),
        out_shape=[jax.ShapeDtypeStruct((slots, 2, BLOCK, HEAD_DIM), jnp.bfloat16)] * (n_ctx - 1),
        in_specs=[SMEM, VMEM, VMEM],
        out_specs=[VMEM] * (n_ctx - 1),
        scratch_shapes=[pltpu.SMEM(((n_ctx - 1) * slots + 1,), jnp.int32)],
        name="gather",
    )(lists, key_states, value_states)


def attend(n_dev, q_ref, out_ref, load_keys, load_values, buffers):
    scores, weights, done, sems = buffers[:2], buffers[2:4], buffers[4], buffers[5]
    heads = HEADS // PARTS

    def lanes(h):
        return slice(h * HEAD_DIM, (h + 1) * HEAD_DIM)

    def rows_of(i):
        return pl.ds(pl.multiple_of(i * BLOCK, BLOCK), BLOCK)

    def form_scores(i, part):
        q = jnp.concatenate([q_ref[rows_of(i), lanes(part * heads + n)] for n in range(heads)], axis=0)
        scores[part % 2][...] = lax.dot_general(
            q, load_keys(i), (((1,), (1,)), ((), ())), preferred_element_type=jnp.float32
        )

    def form_weights(i, part):
        for n in range(heads):
            rows = slice(n * BLOCK, (n + 1) * BLOCK)
            score = scores[part % 2][rows, :]
            top = jnp.max(score, axis=1, keepdims=True)
            weights[part % 2][rows, :] = jnp.exp2((score - top) * TO_LOG2).astype(jnp.bfloat16)

    def sent(i):
        return pltpu.make_async_copy(done.at[rows_of(i)], out_ref.at[rows_of(i)], sems.at[i])

    def sum_up(i, part):
        total = jnp.dot(weights[part % 2][...], load_values(i), preferred_element_type=jnp.float32)
        for n in range(heads):
            rows = slice(n * BLOCK, (n + 1) * BLOCK)
            out = total[rows, :HEAD_DIM] / total[rows, HEAD_DIM:]
            done[rows_of(i), lanes(part * heads + n)] = out.astype(done.dtype)
        if part == PARTS - 1:
            sent(i).start()

    def turn(i, part, before):
        form_scores(i, part)
        for work, lag in ((form_weights, 1), (sum_up, 2)):
            if part >= lag:
                work(i, part - lag)
            elif before is not None:
                work(before, part - lag + PARTS)

    for part in range(PARTS):
        turn(0, part, None)

    def step(u, _):
        for part in range(PARTS):
            turn(u, part, u - 1)
        return 0

    lax.fori_loop(1, n_dev, step, 0)
    form_weights(n_dev - 1, PARTS - 1)
    sum_up(n_dev - 1, PARTS - 2)
    sum_up(n_dev - 1, PARTS - 1)
    for i in range(n_dev):
        sent(i).wait()


def attention_kernel(sizes, where, n_shared, list_ref, q_ref, k_ref, v_ref, before_ref, after_ref, *rest):
    n_pb, n_ctx, n_dev, slots = sizes
    shared_refs, rest = rest[:n_shared], rest[n_shared:]
    parts, (out_ref, pool, table, counts, sems, *buffers) = rest[: len(where)], rest[len(where) :]
    shared = n_dev + 2
    random = shared + GLOBAL
    copies = []
    for n, (part, (at, which)) in enumerate(zip(parts, where)):
        rows = pl.ds(random + at, part.shape[0])
        target = pool.at[rows] if which is None else pool.at[rows, which]
        copies.append(pltpu.make_async_copy(part, target, sems.at[n]))
    for copy in copies:
        copy.start()
    pool[0] = before_ref[0]
    pool[1 : n_dev + 1, 0] = k_ref[...]
    pool[1 : n_dev + 1, 1] = v_ref[...]
    pool[n_dev + 1] = after_ref[0]
    if n_shared == 1:
        pool[shared:random] = shared_refs[0][...]
    else:
        for p in range(n_shared):

            @pl.when(lax.axis_index("pb") == p)
            def _():
                pool[shared:random] = shared_refs[p][...]

    n_blocks = n_pb * n_ctx * n_dev
    me = lax.axis_index("ctx")
    group = lax.axis_index("pb") * (n_ctx * n_dev)
    first = group + me * n_dev

    def brought(block):
        holder = block // n_dev
        away = lax.rem(place_of(me, n_ctx) - place_of(holder, n_ctx) + n_ctx, n_ctx)
        return random + (away - 1) * n_dev + block - holder * n_dev

    ends = (jnp.int32(0), jnp.int32(n_dev + 1))
    if n_ctx == 8:
        own = me * n_dev
        ends = (
            jnp.where(me == 0, 0, brought(jnp.maximum(own - 1, 0))),
            jnp.where(me == n_ctx - 1, n_dev + 1, brought(jnp.minimum(own + n_dev, n_ctx * n_dev - 1))),
        )
    for h in range(n_ctx):
        counts[h] = 0
    for r in range(n_dev):
        row = me * n_dev + r
        start = row * LIST + random_start(group + row, n_blocks)
        for j in range(RANDOM):
            block = list_ref[start + j] - group
            if n_ctx == 8:
                table[r * RANDOM + j] = brought(block)
            else:
                holder = block // n_dev
                rank = counts[holder]
                counts[holder] = rank + 1
                table[r * RANDOM + j] = random + (lax.rem(me - holder + n_ctx, n_ctx) - 1) * slots + rank
    for copy in copies:
        copy.wait()

    def near(i, step):
        block = first + i + step
        place = jnp.where(i + step < 0, ends[0], jnp.where(i + step >= n_dev, ends[1], i + 1 + step))
        return place, jnp.logical_and(block >= GLOBAL, block < n_blocks)

    def load_keys(i):
        places = [shared + g for g in range(GLOBAL)]
        for step in (-1, 0, 1):
            place, use = near(i, step)
            places.append(jnp.where(use, place, shared))
        places += [table[i * RANDOM + j] for j in range(RANDOM)]
        return jnp.concatenate([pool[place, 0] for place in places], axis=0)

    def load_values(i):
        one = jnp.ones((BLOCK, HEAD_DIM), jnp.bfloat16)
        parts = [jnp.concatenate([pool[shared + g, 1], one], axis=1) for g in range(GLOBAL)]
        for step in (-1, 0, 1):
            place, use = near(i, step)
            part = jnp.concatenate([pool[jnp.where(use, place, shared), 1], one], axis=1)
            parts.append(jnp.where(use, part, jnp.zeros_like(part)))
        for j in range(RANDOM):
            parts.append(jnp.concatenate([pool[table[i * RANDOM + j], 1], one], axis=1))
        return jnp.concatenate(parts, axis=0)

    attend(n_dev, q_ref, out_ref, load_keys, load_values, buffers)


def attention(sizes, queries, keys, values, before, after, shared, lists, where, parts):
    n_dev = sizes[2]
    rows, n_keys = HEADS // PARTS * BLOCK, (GLOBAL + 3 + RANDOM) * BLOCK
    n_pool = n_dev + 2 + GLOBAL + max(at + part.shape[0] for part, (at, _) in zip(parts, where))
    return pl.pallas_call(
        lambda *refs: attention_kernel(sizes, where, len(shared), *refs),
        out_shape=jax.ShapeDtypeStruct(queries.shape, jnp.bfloat16),
        in_specs=[SMEM] + [VMEM] * (5 + len(shared)) + [MEM] * len(parts),
        out_specs=MEM,
        scratch_shapes=[
            pltpu.VMEM((n_pool, 2, BLOCK, HEAD_DIM), jnp.bfloat16),
            pltpu.SMEM((n_dev * RANDOM,), jnp.int32),
            pltpu.SMEM((sizes[1],), jnp.int32),
            pltpu.SemaphoreType.DMA((len(parts),)),
            *[pltpu.VMEM((rows, n_keys), jnp.float32)] * 2,
            *[pltpu.VMEM((rows, n_keys), jnp.bfloat16)] * 2,
            pltpu.VMEM(queries.shape, jnp.bfloat16),
            pltpu.SemaphoreType.DMA((n_dev,)),
        ],
        compiler_params=pltpu.CompilerParams(vmem_limit_bytes=24 << 20),
        name="attention",
    )(lists, queries, keys, values, before, after, *shared, *parts)


def shift_round(sizes, lists, keys, values):
    n_ctx = sizes[1]
    return [
        lax.ppermute(part, "ctx", [(i, (i + shift) % n_ctx) for i in range(n_ctx)])
        for shift, part in enumerate(gather(sizes, lists, keys, values), 1)
    ]


def neighbours(first, last):
    axes = ("pb", "ctx")
    n = lax.axis_size(axes)
    up = [(i, i + 1) for i in range(n - 1)]
    down = [(i + 1, i) for i in range(n - 1)]
    return lax.ppermute(last, axes, up), lax.ppermute(first, axes, down)


def spread(shared):
    n_ctx, n_pb = lax.axis_size("ctx"), lax.axis_size("pb")
    column, group = lax.axis_index("ctx"), lax.axis_index("pb")

    def fan(shared, axes, index, targets):
        received = [lax.ppermute(shared, axes, [(0, target)]) for target in targets]
        for target, got in zip(targets, received):
            shared = jnp.where(index == target, got, shared)
        return shared

    shared = fan(shared, ("pb", "ctx"), column, range(2, n_ctx, 2))
    got = lax.ppermute(shared, ("pb", "ctx"), [(c, c + 1) for c in range(0, n_ctx, 2)])
    shared = jnp.where(column % 2 == 1, got, shared)
    return fan(shared, "pb", group, range(1, n_pb))


def per_device(queries, key_states, value_states, key_blocks):
    n_pb, n_ctx = lax.axis_size("pb"), lax.axis_size("ctx")
    n_dev = queries.shape[0] // BLOCK
    slots = (RANDOM * n_dev + n_ctx - 2) // (n_ctx - 1)
    sizes = (n_pb, n_ctx, n_dev, slots)
    keys = key_states.reshape(n_dev, BLOCK, HEAD_DIM)
    values = value_states.reshape(n_dev, BLOCK, HEAD_DIM)
    lists = group_rows(key_blocks)
    first, edge = edges(keys, values)
    if n_ctx == 8:
        last = n_ctx - 1
        direct = lax.ppermute(first, ("pb", "ctx"), [(0, last)])
        across = [(p * n_ctx + last, (p + 1) * n_ctx) for p in range(n_pb - 1)]
        beside = lax.ppermute(edge, ("pb", "ctx"), across + [(b, a) for a, b in across])
        pairs, (direct, lists) = pass_round(keys, values, (direct, lists))
        before = after = beside
        parts = [part for pair in pairs for part in pair]
        where = [(n * n_dev, which) for n in range(n_ctx - 1) for which in range(2)]
        mine = first_of_group(first, direct, pairs)
        shared = [mine] + [lax.ppermute(mine, "pb", [(0, p)]) for p in range(1, n_pb)]
    else:
        parts = shift_round(sizes, lists, keys, values)
        where = [(n * slots, None) for n in range(n_ctx - 1)]
        last = jnp.stack([keys[-1:], values[-1:]], axis=1)
        before, after = neighbours(first[:1], last)
        shared = [spread(first)]
    return attention(sizes, queries, keys, values, before, after, shared, lists, where, parts)


def solution(mesh):
    in_specs = (P(("pb", "ctx"), None), P(("pb", "ctx"), None), P(("pb", "ctx"), None), P())
    out_specs = P(("pb", "ctx"), None)
    return jax.shard_map(
        per_device, mesh=mesh, in_specs=in_specs, out_specs=out_specs, check_vma=False
    )
```

```python
import jax
import jax.numpy as jnp
from jax import lax
from jax.experimental import pallas as pl
from jax.experimental.pallas import tpu as pltpu
from jax.sharding import PartitionSpec as P

HEAD_DIM = 128
HEADS = 8
BLOCK = 128
GLOBAL = 2
RANDOM = 3
LIST = 8
PARTS = 4
TO_LOG2 = HEAD_DIM**-0.5 * 1.4426950408889634

VMEM = pl.BlockSpec(memory_space=pltpu.VMEM)
MEM = pl.BlockSpec(memory_space=pltpu.HBM)
SMEM = pl.BlockSpec(memory_space=pltpu.SMEM)


def random_start(row, n_blocks):
    low = jnp.maximum(row - 1, GLOBAL)
    high = jnp.minimum(row + 1, n_blocks - 1)
    return GLOBAL + high - low + 1


def group_rows(key_blocks):
    n_rows = key_blocks.shape[0] // lax.axis_size("pb")
    return lax.dynamic_slice_in_dim(
        key_blocks, lax.axis_index("pb") * n_rows, n_rows, 0
    ).reshape(-1)


def ring_of(n_ctx):
    return list(range(0, n_ctx, 2)) + list(range(n_ctx - 1, 0, -2))


def place_of(index, n_ctx):
    return jnp.where(index % 2 == 0, index // 2, n_ctx - 1 - index // 2)


def edges(keys, values):
    n_dev = keys.shape[0]

    def kernel(k_ref, v_ref, first_ref, edge_ref, sems):
        last = lax.axis_index("ctx") == lax.axis_size("ctx") - 1
        edge = pl.ds(jnp.where(last, n_dev - 1, 0), 1)
        copies = []
        for which, ref in enumerate((k_ref, v_ref)):
            copies += [
                pltpu.make_async_copy(ref.at[pl.ds(0, GLOBAL)], first_ref.at[:, which], sems.at[2 * which]),
                pltpu.make_async_copy(ref.at[edge], edge_ref.at[:, which], sems.at[2 * which + 1]),
            ]
        for copy in copies:
            copy.start()
        for copy in copies:
            copy.wait()

    return pl.pallas_call(
        kernel,
        out_shape=[jax.ShapeDtypeStruct((n, 2, BLOCK, HEAD_DIM), jnp.bfloat16) for n in (GLOBAL, 1)],
        in_specs=[MEM, MEM],
        out_specs=[VMEM, VMEM],
        scratch_shapes=[pltpu.SemaphoreType.DMA((4,))],
        compiler_params=pltpu.CompilerParams(vmem_limit_bytes=2 << 20),
        name="edges",
    )(keys, values)


def first_of_group(first, direct, pairs):
    def kernel(*refs):
        *parts, out_ref, sems = refs
        place = place_of(lax.axis_index("ctx"), lax.axis_size("ctx"))
        for at, n in enumerate((0, 4)):

            @pl.when(place == n)
            def _():
                copy = pltpu.make_async_copy(parts[at], out_ref, sems.at[0])
                copy.start()
                copy.wait()

        for n, away in enumerate(whole):

            @pl.when(place == away)
            def _():
                copies = [
                    pltpu.make_async_copy(
                        parts[2 + 2 * n + which].at[pl.ds(0, GLOBAL)], out_ref.at[:, which], sems.at[which]
                    )
                    for which in range(2)
                ]
                for copy in copies:
                    copy.start()
                for copy in copies:
                    copy.wait()

    whole = [away for away in range(1, 8) if away != 4]
    parts = [first, direct] + [part for away in whole for part in pairs[away - 1]]
    return pl.pallas_call(
        kernel,
        out_shape=jax.ShapeDtypeStruct(first.shape, jnp.bfloat16),
        in_specs=[MEM] * len(parts),
        out_specs=VMEM,
        scratch_shapes=[pltpu.SemaphoreType.DMA((2,))],
        compiler_params=pltpu.CompilerParams(vmem_limit_bytes=2 << 20),
        name="first",
    )(*parts)


def pass_round(keys, values, small):
    n_ctx = lax.axis_size("ctx")
    ring = ring_of(n_ctx)
    ahead = [(ring[i], ring[(i + 1) % n_ctx]) for i in range(n_ctx)]
    back = [(b, a) for a, b in ahead]
    parts = {}
    k = [keys, keys]
    v = [values, values]
    for hop in range(1, n_ctx // 2):
        if hop == n_ctx // 2 - 1:
            k[0], small = lax.optimization_barrier((k[0], small))
        for side, pairs in enumerate((ahead, back)):
            k[side] = lax.ppermute(k[side], "ctx", pairs)
        for side, pairs in enumerate((ahead, back)):
            v[side] = lax.ppermute(v[side], "ctx", pairs)
        parts[hop], parts[n_ctx - hop] = (k[0], v[0]), (k[1], v[1])
    parts[n_ctx // 2] = (lax.ppermute(k[0], "ctx", ahead), lax.ppermute(v[1], "ctx", back))
    return [parts[away] for away in range(1, n_ctx)], small


def gather_kernel(sizes, list_ref, k_ref, v_ref, *rest):
    n_pb, n_ctx, n_dev, slots = sizes
    outs, table = rest[:-1], rest[-1]
    n_blocks = n_pb * n_ctx * n_dev
    me = lax.axis_index("ctx")
    group = lax.axis_index("pb") * (n_ctx * n_dev)
    own = group + me * n_dev
    for i in range((n_ctx - 1) * slots + 1):
        table[i] = 0
    for shift in range(1, n_ctx):
        first = lax.rem(me + shift, n_ctx) * n_dev
        count = jnp.int32(0)
        for r in range(n_dev):
            row = first + r
            start = row * LIST + random_start(group + row, n_blocks)
            for j in range(RANDOM):
                local = list_ref[start + j] - own
                hit = jnp.logical_and(local >= 0, local < n_dev)
                place = jnp.where(hit, (shift - 1) * slots + count, (n_ctx - 1) * slots)
                table[place] = local
                count = count + hit.astype(jnp.int32)
    for shift in range(1, n_ctx):
        for s in range(slots):
            local = table[(shift - 1) * slots + s]
            outs[shift - 1][s, 0] = k_ref[local]
            outs[shift - 1][s, 1] = v_ref[local]


def gather(sizes, lists, key_states, value_states):
    n_pb, n_ctx, n_dev, slots = sizes
    return pl.pallas_call(
        lambda *refs: gather_kernel(sizes, *refs),
        out_shape=[jax.ShapeDtypeStruct((slots, 2, BLOCK, HEAD_DIM), jnp.bfloat16)] * (n_ctx - 1),
        in_specs=[SMEM, VMEM, VMEM],
        out_specs=[VMEM] * (n_ctx - 1),
        scratch_shapes=[pltpu.SMEM(((n_ctx - 1) * slots + 1,), jnp.int32)],
        name="gather",
    )(lists, key_states, value_states)


def attend(n_dev, q_ref, out_ref, load_keys, load_values, late, buffers):
    scores, weights, done, sems = buffers[:2], buffers[2:4], buffers[4], buffers[5]
    heads = HEADS // PARTS

    def lanes(h):
        return slice(h * HEAD_DIM, (h + 1) * HEAD_DIM)

    def rows_of(i):
        return pl.ds(pl.multiple_of(i * BLOCK, BLOCK), BLOCK)

    def form_scores(i, part):
        q = jnp.concatenate([q_ref[rows_of(i), lanes(part * heads + n)] for n in range(heads)], axis=0)
        scores[part % 2][...] = lax.dot_general(
            q, load_keys(i), (((1,), (1,)), ((), ())), preferred_element_type=jnp.float32
        )

    def form_weights(i, part):
        for n in range(heads):
            rows = slice(n * BLOCK, (n + 1) * BLOCK)
            score = scores[part % 2][rows, :]
            top = jnp.max(score, axis=1, keepdims=True)
            weights[part % 2][rows, :] = jnp.exp2((score - top) * TO_LOG2).astype(jnp.bfloat16)

    def sent(i):
        return pltpu.make_async_copy(done.at[rows_of(i)], out_ref.at[rows_of(i)], sems.at[i])

    def sum_up(i, part):
        total = jnp.dot(weights[part % 2][...], load_values(i), preferred_element_type=jnp.float32)
        for n in range(heads):
            rows = slice(n * BLOCK, (n + 1) * BLOCK)
            out = total[rows, :HEAD_DIM] / total[rows, HEAD_DIM:]
            done[rows_of(i), lanes(part * heads + n)] = out.astype(done.dtype)
        if part == PARTS - 1:
            sent(i).start()

    def turn(i, part, before):
        form_scores(i, part)
        for work, lag in ((form_weights, 1), (sum_up, 2)):
            if part >= lag:
                work(i, part - lag)
            elif before is not None:
                work(before, part - lag + PARTS)

    for part in range(PARTS):
        if part == 2:
            for copy in late:
                copy.wait()
        turn(0, part, None)

    def step(u, _):
        for part in range(PARTS):
            turn(u, part, u - 1)
        return 0

    lax.fori_loop(1, n_dev, step, 0)
    form_weights(n_dev - 1, PARTS - 1)
    sum_up(n_dev - 1, PARTS - 2)
    sum_up(n_dev - 1, PARTS - 1)
    for i in range(n_dev):
        sent(i).wait()


def attention_kernel(sizes, where, n_shared, list_ref, q_ref, k_ref, v_ref, before_ref, after_ref, *rest):
    n_pb, n_ctx, n_dev, slots = sizes
    shared_refs, rest = rest[:n_shared], rest[n_shared:]
    parts, (out_ref, pool, table, counts, sems, *buffers) = rest[: len(where)], rest[len(where) :]
    shared = n_dev + 2
    random = shared + GLOBAL
    copies = []
    for n, (part, (at, which)) in enumerate(zip(parts, where)):
        rows = pl.ds(random + at, part.shape[0])
        target = pool.at[rows] if which is None else pool.at[rows, which]
        copies.append(pltpu.make_async_copy(part, target, sems.at[n]))
    for copy in copies:
        copy.start()
    pool[0] = before_ref[0]
    pool[1 : n_dev + 1, 0] = k_ref[...]
    pool[1 : n_dev + 1, 1] = v_ref[...]
    pool[n_dev + 1] = after_ref[0]
    if n_shared == 1:
        pool[shared:random] = shared_refs[0][...]
    else:
        for p in range(n_shared):

            @pl.when(lax.axis_index("pb") == p)
            def _():
                pool[shared:random] = shared_refs[p][...]

    n_blocks = n_pb * n_ctx * n_dev
    me = lax.axis_index("ctx")
    group = lax.axis_index("pb") * (n_ctx * n_dev)
    first = group + me * n_dev

    def brought(block):
        holder = block // n_dev
        away = lax.rem(place_of(me, n_ctx) - place_of(holder, n_ctx) + n_ctx, n_ctx)
        return random + (away - 1) * n_dev + block - holder * n_dev

    ends = (jnp.int32(0), jnp.int32(n_dev + 1))
    if n_ctx == 8:
        own = me * n_dev
        ends = (
            jnp.where(me == 0, 0, brought(jnp.maximum(own - 1, 0))),
            jnp.where(me == n_ctx - 1, n_dev + 1, brought(jnp.minimum(own + n_dev, n_ctx * n_dev - 1))),
        )
    for h in range(n_ctx):
        counts[h] = 0
    for r in range(n_dev):
        row = me * n_dev + r
        start = row * LIST + random_start(group + row, n_blocks)
        for j in range(RANDOM):
            block = list_ref[start + j] - group
            if n_ctx == 8:
                table[r * RANDOM + j] = brought(block)
            else:
                holder = block // n_dev
                rank = counts[holder]
                counts[holder] = rank + 1
                table[r * RANDOM + j] = random + (lax.rem(me - holder + n_ctx, n_ctx) - 1) * slots + rank
    late = [copy for copy, (_, which) in zip(copies, where) if which == 1]
    for copy, (_, which) in zip(copies, where):
        if which != 1:
            copy.wait()

    def near(i, step):
        block = first + i + step
        place = jnp.where(i + step < 0, ends[0], jnp.where(i + step >= n_dev, ends[1], i + 1 + step))
        return place, jnp.logical_and(block >= GLOBAL, block < n_blocks)

    def load_keys(i):
        places = [shared + g for g in range(GLOBAL)]
        for step in (-1, 0, 1):
            place, use = near(i, step)
            places.append(jnp.where(use, place, shared))
        places += [table[i * RANDOM + j] for j in range(RANDOM)]
        return jnp.concatenate([pool[place, 0] for place in places], axis=0)

    def load_values(i):
        one = jnp.ones((BLOCK, HEAD_DIM), jnp.bfloat16)
        parts = [jnp.concatenate([pool[shared + g, 1], one], axis=1) for g in range(GLOBAL)]
        for step in (-1, 0, 1):
            place, use = near(i, step)
            part = jnp.concatenate([pool[jnp.where(use, place, shared), 1], one], axis=1)
            parts.append(jnp.where(use, part, jnp.zeros_like(part)))
        for j in range(RANDOM):
            parts.append(jnp.concatenate([pool[table[i * RANDOM + j], 1], one], axis=1))
        return jnp.concatenate(parts, axis=0)

    attend(n_dev, q_ref, out_ref, load_keys, load_values, late, buffers)


def attention(sizes, queries, keys, values, before, after, shared, lists, where, parts):
    n_dev = sizes[2]
    rows, n_keys = HEADS // PARTS * BLOCK, (GLOBAL + 3 + RANDOM) * BLOCK
    n_pool = n_dev + 2 + GLOBAL + max(at + part.shape[0] for part, (at, _) in zip(parts, where))
    return pl.pallas_call(
        lambda *refs: attention_kernel(sizes, where, len(shared), *refs),
        out_shape=jax.ShapeDtypeStruct(queries.shape, jnp.bfloat16),
        in_specs=[SMEM] + [VMEM] * (5 + len(shared)) + [MEM] * len(parts),
        out_specs=MEM,
        scratch_shapes=[
            pltpu.VMEM((n_pool, 2, BLOCK, HEAD_DIM), jnp.bfloat16),
            pltpu.SMEM((n_dev * RANDOM,), jnp.int32),
            pltpu.SMEM((sizes[1],), jnp.int32),
            pltpu.SemaphoreType.DMA((len(parts),)),
            *[pltpu.VMEM((rows, n_keys), jnp.float32)] * 2,
            *[pltpu.VMEM((rows, n_keys), jnp.bfloat16)] * 2,
            pltpu.VMEM(queries.shape, jnp.bfloat16),
            pltpu.SemaphoreType.DMA((n_dev,)),
        ],
        compiler_params=pltpu.CompilerParams(vmem_limit_bytes=24 << 20),
        name="attention",
    )(lists, queries, keys, values, before, after, *shared, *parts)


def shift_round(sizes, lists, keys, values):
    n_ctx = sizes[1]
    return [
        lax.ppermute(part, "ctx", [(i, (i + shift) % n_ctx) for i in range(n_ctx)])
        for shift, part in enumerate(gather(sizes, lists, keys, values), 1)
    ]


def neighbours(first, last):
    axes = ("pb", "ctx")
    n = lax.axis_size(axes)
    up = [(i, i + 1) for i in range(n - 1)]
    down = [(i + 1, i) for i in range(n - 1)]
    return lax.ppermute(last, axes, up), lax.ppermute(first, axes, down)


def spread(shared):
    n_ctx, n_pb = lax.axis_size("ctx"), lax.axis_size("pb")
    column, group = lax.axis_index("ctx"), lax.axis_index("pb")

    def fan(shared, axes, index, targets):
        received = [lax.ppermute(shared, axes, [(0, target)]) for target in targets]
        for target, got in zip(targets, received):
            shared = jnp.where(index == target, got, shared)
        return shared

    shared = fan(shared, ("pb", "ctx"), column, range(2, n_ctx, 2))
    got = lax.ppermute(shared, ("pb", "ctx"), [(c, c + 1) for c in range(0, n_ctx, 2)])
    shared = jnp.where(column % 2 == 1, got, shared)
    return fan(shared, "pb", group, range(1, n_pb))


def per_device(queries, key_states, value_states, key_blocks):
    n_pb, n_ctx = lax.axis_size("pb"), lax.axis_size("ctx")
    n_dev = queries.shape[0] // BLOCK
    slots = (RANDOM * n_dev + n_ctx - 2) // (n_ctx - 1)
    sizes = (n_pb, n_ctx, n_dev, slots)
    keys = key_states.reshape(n_dev, BLOCK, HEAD_DIM)
    values = value_states.reshape(n_dev, BLOCK, HEAD_DIM)
    lists = group_rows(key_blocks)
    first, edge = edges(keys, values)
    if n_ctx == 8:
        last = n_ctx - 1
        direct = lax.ppermute(first, ("pb", "ctx"), [(0, last)])
        across = [(p * n_ctx + last, (p + 1) * n_ctx) for p in range(n_pb - 1)]
        beside = lax.ppermute(edge, ("pb", "ctx"), across + [(b, a) for a, b in across])
        pairs, (direct, lists) = pass_round(keys, values, (direct, lists))
        before = after = beside
        parts = [part for pair in pairs for part in pair]
        where = [(n * n_dev, which) for n in range(n_ctx - 1) for which in range(2)]
        mine = first_of_group(first, direct, pairs)
        shared = [mine] + [lax.ppermute(mine, "pb", [(0, p)]) for p in range(1, n_pb)]
    else:
        parts = shift_round(sizes, lists, keys, values)
        where = [(n * slots, None) for n in range(n_ctx - 1)]
        last = jnp.stack([keys[-1:], values[-1:]], axis=1)
        before, after = neighbours(first[:1], last)
        shared = [spread(first)]
    return attention(sizes, queries, keys, values, before, after, shared, lists, where, parts)


def solution(mesh):
    in_specs = (P(("pb", "ctx"), None), P(("pb", "ctx"), None), P(("pb", "ctx"), None), P())
    out_specs = P(("pb", "ctx"), None)
    return jax.shard_map(
        per_device, mesh=mesh, in_specs=in_specs, out_specs=out_specs, check_vma=False
    )
```
